32 devices in a mesh: dp: 8 (over y, x, core), tensor: 4 (over z).
Axes of the slice: x: 2, y: 2, z: 4, core: 2. Of those that a mesh axis runs over, the one named last changes fastest.
Arguments:
- inputs: float32 [8, 1376, 1024], P('dp', 'tensor'), may hold values from -8 to 8
- grad_output: float32 [8, 1376, 1024], P('dp', 'tensor'), may hold values from -6 to 6
- valid_count: int32 [8], P('dp'), may hold values from 688 to 1376, as said below
- attend_weight: bfloat16 [3, 1024, 1024], P(None, 'dp', 'tensor'), may hold values from -0.75 to 0.75
- attend_bias: bfloat16 [2, 1024], P(None, ('tensor', 'dp')), may hold values from -3 to 3
- merge_weight: bfloat16 [1024, 1024], P('tensor', 'dp'), may hold values from -0.5 to 0.5
- expand_weight: bfloat16 [1024, 4096], P('dp', 'tensor'), may hold values from -0.1875 to 0.1875
- expand_bias: bfloat16 [4096], P(('tensor', 'dp')), may hold values from -3 to 3
- reduce_weight: bfloat16 [4096, 1024], P('tensor', 'dp'), may hold values from -0.09375 to 0.09375
- norm_gains: float32 [2, 1024], P(None, ('dp', 'tensor')), may hold values from 0.5 to 1.5
- norm_shifts: float32 [2, 1024], P(None, ('dp', 'tensor')), may hold values from -3 to 3
- layer_scales: float32 [2, 1024], P(None, ('dp', 'tensor')), may hold values from 0.3 to 1.5
- branch_biases: float32 [2, 1024], P(None, ('dp', 'tensor')), may hold values from -3 to 3
Outputs:
- layer_output: float32 [8, 1376, 1024], P('dp', 'tensor')
- input_grad: float32 [8, 1376, 1024], P('dp', 'tensor')
- attend_weight_grad: float32 [3, 1024, 1024], P(None, 'dp', 'tensor')
- attend_bias_grad: float32 [2, 1024], P(None, ('tensor', 'dp'))
- merge_weight_grad: float32 [1024, 1024], P('tensor', 'dp')
- expand_weight_grad: float32 [1024, 4096], P('dp', 'tensor')
- expand_bias_grad: float32 [4096], P(('tensor', 'dp'))
- reduce_weight_grad: float32 [4096, 1024], P('tensor', 'dp')
- norm_gains_grad: float32 [2, 1024], P(None, ('dp', 'tensor'))
- norm_shifts_grad: float32 [2, 1024], P(None, ('dp', 'tensor'))
- layer_scales_grad: float32 [2, 1024], P(None, ('dp', 'tensor'))
- branch_biases_grad: float32 [2, 1024], P(None, ('dp', 'tensor'))
The draws below stay inside these ranges and needn't reach their ends.
Inputs may be any that keep to these rules, and one draw needn't show every extreme that they name: An image attends to its first valid_count key positions; in every draw some image has 1376 and some 1376 // 2.
All inputs are finite; a program needn't handle non-finite values.
Results may differ from the reference program's by a relative error of at most 0.033.
The reference program's roundings to bfloat16 on the way count: a program that leaves them out, or rounds other values in their place, can miss the bound.
Values may be sent and summed in bfloat16 or wider, within the bound.
No kernel may reach another device: no remote copies, remote signals or barrier semaphores. Data moves between devices by JAX's collectives and lax.ppermute only.
A program may use at most 192 MiB of HBM per device.

```python
import math
import jax
import jax.numpy as jnp
from jax import lax

D = 1024
HEADS = 16
HEAD_DIM = 64
FF = 4096
SEQ = 1376
IMAGES = 8


def draw_valid_count(key, part):
    first_key, second_key = jax.random.split(jax.random.fold_in(key, 11))
    counts = jax.random.randint(first_key, (IMAGES,), SEQ // 2, SEQ + 1, dtype=jnp.int32)
    chosen = jax.random.randint(second_key, (), 0, IMAGES, dtype=jnp.int32)
    position = jnp.arange(IMAGES, dtype=jnp.int32)
    counts = jnp.where(position == chosen, SEQ, counts)
    counts = jnp.where(position == (chosen + 1) % IMAGES, SEQ // 2, counts)
    return counts.astype(jnp.int32)


def draw_inputs(key, part):
    random_key = jax.random.fold_in(jax.random.fold_in(key, 3), 0)
    return jax.random.truncated_normal(random_key, -6.0, 6.0, (IMAGES, SEQ, D), jnp.float32)


def draw_attend_weight(key, part):
    base_key = jax.random.fold_in(key, 5)
    base_matrix = jax.random.truncated_normal(base_key, -6.0, 6.0, (3, D, D), jnp.float32) / math.sqrt(D)
    return base_matrix.astype(jnp.bfloat16)


def shard_levels(rng, dims, pieces, smallest, top_value):
    loudness = 1.0
    for dim, blocks in pieces:
        draws = jax.random.uniform(jax.random.fold_in(jax.random.fold_in(rng, 6), dim), (blocks,), jnp.float32, smallest / len(pieces), top_value / len(pieces))
        loudness = loudness * jnp.repeat(jnp.exp(draws), dims[dim] // blocks).reshape((-1,) + (1,) * (len(dims) - 1 - dim))
    return loudness


def noise(own_key, extent, scale, limit, cuts=(), held_as=jnp.bfloat16):
    result = jax.random.normal(own_key, extent, jnp.float32) * scale
    if len(cuts) > 0:
        result = shard_levels(own_key, extent, cuts, -0.22, 0.18) * result
    return jnp.clip(result, min=-limit, max=limit).astype(held_as)


def setup_inputs(seed: int = 0) -> dict:
    key_list = jax.random.split(jax.random.key(seed), 14)
    return {
        "inputs": draw_inputs(jax.random.fold_in(key_list[13], 71), 0),
        "grad_output": noise(key_list[1], (IMAGES, SEQ, D), 1.0, 6.0, ((0, 8), (1, 4)), jnp.float32),
        "valid_count": draw_valid_count(jax.random.fold_in(key_list[13], 71), 0),
        "attend_weight": draw_attend_weight(jax.random.fold_in(key_list[13], 71), 0),
        "attend_bias": noise(key_list[4], (2, D), 0.5, 3.0, ((1, 32),)),
        "merge_weight": noise(key_list[5], (D, D), (D // 8) ** -0.5, 0.5, ((0, 4), (1, 8))),
        "expand_weight": noise(key_list[6], (D, FF), D ** -0.5, 0.1875, ((0, 8), (1, 4))),
        "expand_bias": noise(key_list[7], (FF,), 0.5, 3.0, ((0, 32),)),
        "reduce_weight": noise(key_list[8], (FF, D), FF ** -0.5, 0.09375, ((0, 4), (1, 8))),
        "norm_gains": jnp.clip(1.0 + 0.1 * jax.random.normal(key_list[9], (2, D), jnp.float32), 0.5, 1.5),
        "norm_shifts": noise(key_list[10], (2, D), 0.5, 3.0, ((1, 32),), jnp.float32),
        "layer_scales": jnp.clip(jnp.exp(math.log(1.5) - 1.60943787 * jax.random.uniform(key_list[11], (2, D), jnp.float32) ** shard_levels(key_list[11], (2, D), ((1, 32),), -0.2, 0.2)), 0.3, 1.5),
        "branch_biases": noise(key_list[12], (2, D), 0.5, 3.0, ((1, 32),), jnp.float32),
    }


EPSILON = 1e-06
BIG_NEG = -1e+30

def standardize(rows_in):
    centered = rows_in - lax.optimization_barrier(jnp.mean(rows_in, axis=-1, keepdims=True))
    inverse = lax.rsqrt(lax.optimization_barrier(jnp.mean(centered * centered, axis=-1, keepdims=True)) + EPSILON)
    return (centered * inverse, inverse)

def norm_back(grad_rows, scaled, inverse, norm_gain):
    grad_scaled = grad_rows * norm_gain
    return inverse * (grad_scaled - lax.optimization_barrier(jnp.mean(grad_scaled, axis=-1, keepdims=True)) - scaled * lax.optimization_barrier(jnp.mean(grad_scaled * scaled, axis=-1, keepdims=True)))

def gelu_slope(pre_act):
    return 0.5 * (1.0 + lax.erf(pre_act * 0.7071067811865476)) + pre_act * jnp.exp(-0.5 * pre_act * pre_act) * 0.3989422804014327

def masked_scores(queries, key_rows, key_count):
    length = queries.shape[0]
    raw_scores = jnp.einsum('qhd,khd->hqk', queries.astype(jnp.float32), key_rows.astype(jnp.float32)) * queries.shape[2] ** (-0.5)
    keep_mask = jnp.arange(length, dtype=jnp.int32)[None, None, :] < key_count
    return jnp.where(keep_mask, raw_scores, BIG_NEG)

def attend(queries, key_rows, value_rows, key_count):
    scores = masked_scores(queries, key_rows, key_count)
    maximum = lax.optimization_barrier(jnp.max(scores, axis=-1, keepdims=True))
    raised = jnp.exp(scores - maximum)
    totals = lax.optimization_barrier(jnp.sum(raised, axis=-1, keepdims=True))
    attn_probs = (raised / totals).astype(jnp.bfloat16)
    mixed = jnp.einsum('hqk,khd->qhd', attn_probs.astype(jnp.float32), value_rows.astype(jnp.float32)).astype(jnp.bfloat16)
    return (mixed, maximum + jnp.log(totals))

def attend_back(queries, key_rows, value_rows, mixed, grad_mixed, log_total, key_count):
    scores = masked_scores(queries, key_rows, key_count)
    probs_back = jnp.exp(scores - log_total)
    probs_low = probs_back.astype(jnp.bfloat16)
    grad_wide = grad_mixed.astype(jnp.float32)
    grad_values = jnp.einsum('hqk,qhd->khd', probs_low.astype(jnp.float32), grad_wide)
    grad_probs = jnp.einsum('qhd,khd->hqk', grad_wide, value_rows.astype(jnp.float32))
    row_dots = jnp.transpose(lax.optimization_barrier(jnp.sum(grad_wide * mixed.astype(jnp.float32), axis=-1)))[:, :, None]
    grad_scores = (probs_back * (grad_probs - row_dots)).astype(jnp.bfloat16).astype(jnp.float32)
    score_scale = queries.shape[2] ** (-0.5)
    grad_queries = jnp.einsum('hqk,khd->qhd', grad_scores, key_rows.astype(jnp.float32)) * score_scale
    grad_keys = jnp.einsum('hqk,qhd->khd', grad_scores, queries.astype(jnp.float32)) * score_scale
    return (grad_queries, grad_keys, grad_values)

def reference(inputs, grad_output, valid_count, attend_weight, attend_bias, merge_weight, expand_weight, expand_bias, reduce_weight, norm_gains, norm_shifts, layer_scales, branch_biases):
    bias_three = jnp.stack([attend_bias[0].astype(jnp.float32), jnp.zeros((D,), jnp.float32), attend_bias[1].astype(jnp.float32)])

    def split_heads(flat):
        return flat.reshape(SEQ, HEADS, HEAD_DIM)

    def one_image(totals, item):
        image_in, image_grad, key_count = item
        scaled_one, inverse_one = standardize(image_in)
        rows_one = (scaled_one * norm_gains[0] + norm_shifts[0]).astype(jnp.bfloat16)
        projected = jnp.stack([jnp.dot(rows_one, attend_weight[member], preferred_element_type=jnp.float32) for member in range(3)]) + bias_three[:, None, :]
        projected = projected.astype(jnp.bfloat16)
        queries = split_heads(projected[0])
        key_rows = split_heads(projected[1])
        value_rows = split_heads(projected[2])
        mixed, log_total = attend(queries, key_rows, value_rows, key_count)
        mixed_flat = mixed.reshape(SEQ, D)
        branch_one = jnp.dot(mixed_flat, merge_weight, preferred_element_type=jnp.float32) + branch_biases[0]
        middle = image_in + layer_scales[0] * branch_one
        scaled_two, inverse_two = standardize(middle)
        rows_two = (scaled_two * norm_gains[1] + norm_shifts[1]).astype(jnp.bfloat16)
        pre_act = jnp.dot(rows_two, expand_weight, preferred_element_type=jnp.float32) + expand_bias.astype(jnp.float32)
        hidden = jax.nn.gelu(pre_act, approximate=False).astype(jnp.bfloat16)
        branch_two = jnp.dot(hidden, reduce_weight, preferred_element_type=jnp.float32) + branch_biases[1]
        image_out = middle + layer_scales[1] * branch_two
        grad_two = (image_grad * layer_scales[1]).astype(jnp.bfloat16)
        reduce_part = jnp.dot(hidden.T, grad_two, preferred_element_type=jnp.float32)
        grad_pre = jnp.dot(grad_two, reduce_weight.T, preferred_element_type=jnp.float32) * gelu_slope(pre_act)
        grad_pre_low = grad_pre.astype(jnp.bfloat16)
        expand_part = jnp.dot(rows_two.T, grad_pre_low, preferred_element_type=jnp.float32)
        expand_bias_part = lax.optimization_barrier(jnp.sum(grad_pre, axis=0))
        grad_norm_two = jnp.dot(grad_pre_low, expand_weight.T, preferred_element_type=jnp.float32)
        grad_middle = image_grad + norm_back(grad_norm_two, scaled_two, inverse_two, norm_gains[1])
        grad_one = (grad_middle * layer_scales[0]).astype(jnp.bfloat16)
        merge_part = jnp.dot(mixed_flat.T, grad_one, preferred_element_type=jnp.float32)
        grad_mixed = jnp.dot(grad_one, merge_weight.T, preferred_element_type=jnp.float32).astype(jnp.bfloat16)
        grad_queries, grad_keys, grad_values = attend_back(queries, key_rows, value_rows, mixed, split_heads(grad_mixed), log_total, key_count)
        grad_stack = jnp.stack([grad_queries.reshape(SEQ, D), grad_keys.reshape(SEQ, D), grad_values.reshape(SEQ, D)])
        grad_low = grad_stack.astype(jnp.bfloat16)
        attend_part = jnp.stack([jnp.dot(rows_one.T, grad_low[member], preferred_element_type=jnp.float32) for member in range(3)])
        attend_bias_part = jnp.stack([lax.optimization_barrier(jnp.sum(grad_stack[0], axis=0)), lax.optimization_barrier(jnp.sum(grad_stack[2], axis=0))])
        grad_norm_one = jnp.dot(grad_low[0], attend_weight[0].T, preferred_element_type=jnp.float32) + jnp.dot(grad_low[1], attend_weight[1].T, preferred_element_type=jnp.float32) + jnp.dot(grad_low[2], attend_weight[2].T, preferred_element_type=jnp.float32)
        image_in_grad = grad_middle + norm_back(grad_norm_one, scaled_one, inverse_one, norm_gains[0])
        gains_part = jnp.stack([lax.optimization_barrier(jnp.sum(grad_norm_one * scaled_one, axis=0)), lax.optimization_barrier(jnp.sum(grad_norm_two * scaled_two, axis=0))])
        shifts_part = jnp.stack([lax.optimization_barrier(jnp.sum(grad_norm_one, axis=0)), lax.optimization_barrier(jnp.sum(grad_norm_two, axis=0))])
        scales_part = jnp.stack([lax.optimization_barrier(jnp.sum(grad_middle * branch_one, axis=0)), lax.optimization_barrier(jnp.sum(image_grad * branch_two, axis=0))])
        biases_part = jnp.stack([lax.optimization_barrier(jnp.sum(grad_middle * layer_scales[0], axis=0)), lax.optimization_barrier(jnp.sum(image_grad * layer_scales[1], axis=0))])
        parts = (attend_part, attend_bias_part, merge_part, expand_part, expand_bias_part, reduce_part, gains_part, shifts_part, scales_part, biases_part)
        totals = jax.tree.map(jnp.add, totals, parts)
        return (totals, (image_out, image_in_grad))
    start = (jnp.zeros((3, D, D), jnp.float32), jnp.zeros((2, D), jnp.float32), jnp.zeros((D, D), jnp.float32), jnp.zeros((D, FF), jnp.float32), jnp.zeros((FF,), jnp.float32), jnp.zeros((FF, D), jnp.float32), jnp.zeros((2, D), jnp.float32), jnp.zeros((2, D), jnp.float32), jnp.zeros((2, D), jnp.float32), jnp.zeros((2, D), jnp.float32))
    totals, stacked = lax.scan(one_image, start, (inputs, grad_output, valid_count))
    layer_output, input_grad = stacked
    grad_scale = 1.0 / math.sqrt(IMAGES * SEQ)
    totals = [part * grad_scale for part in totals]
    return (layer_output, input_grad, totals[0], totals[1], totals[2], totals[3], totals[4], totals[5], totals[6], totals[7], totals[8], totals[9])
```

```python
import math

import jax
import jax.numpy as jnp
from jax import lax
from jax.sharding import Mesh, PartitionSpec as P

HEAD_DIM = 64
EPSILON = 1e-06
BIG_NEG = -1e30
BF16 = jnp.bfloat16
F32 = jnp.float32


def swap(value, axis, size, distance):
    return lax.ppermute(value, axis, [(i, i ^ distance) for i in range(size)])


def gather_relative(value, axis, size):
    return [value] + [swap(value, axis, size, s) for s in range(1, size)]


def exchange(chunks, axis, size):
    return [chunks[0]] + [swap(chunks[s], axis, size, s) for s in range(1, size)]


def add_up(chunks):
    total = chunks[0].astype(F32)
    for chunk in chunks[1:]:
        total = total + chunk.astype(F32)
    return total


def gather_line(value, size):
    if size != 4:
        return gather_relative(value, "tensor", size)
    two = swap(value, "tensor", 4, 2)
    one = swap(value, "tensor", 4, 1)
    inner = lax.ppermute(value, "tensor", [(1, 2), (2, 1)])
    outer = lax.ppermute(two, "tensor", [(2, 3), (1, 0)])
    place = lax.axis_index("tensor")
    three = jnp.where((place == 1) | (place == 2), inner, outer)
    return [value, one, two, three]


def standardize(rows_in):
    centered = rows_in - jnp.mean(rows_in, axis=-1, keepdims=True)
    inverse = lax.rsqrt(jnp.mean(centered * centered, axis=-1, keepdims=True) + EPSILON)
    return (centered * inverse, inverse)


def norm_back(grad_rows, scaled, inverse, norm_gain):
    grad_scaled = grad_rows * norm_gain
    return inverse * (
        grad_scaled
        - jnp.mean(grad_scaled, axis=-1, keepdims=True)
        - scaled * jnp.mean(grad_scaled * scaled, axis=-1, keepdims=True)
    )


def gelu_slope(pre_act):
    return (
        0.5 * (1.0 + lax.erf(pre_act * 0.7071067811865476))
        + pre_act * jnp.exp(-0.5 * pre_act * pre_act) * 0.3989422804014327
    )


def dot(left, right, left_dim, right_dim):
    return lax.dot_general(
        left, right, (((left_dim,), (right_dim,)), ((), ())), preferred_element_type=F32
    )


def split_heads(flat):
    return flat.reshape(flat.shape[0], flat.shape[1] // HEAD_DIM, HEAD_DIM)


def masked_scores(queries, key_rows, keep):
    raw = jnp.einsum("qhd,khd->hqk", queries, key_rows, preferred_element_type=F32)
    return jnp.where(keep[None, None, :], raw * HEAD_DIM ** (-0.5), BIG_NEG)


def attend(query_flat, key_flat, value_flat, keep):
    scores = masked_scores(split_heads(query_flat), split_heads(key_flat), keep)
    maximum = jnp.max(scores, axis=-1, keepdims=True)
    raised = jnp.exp(scores - maximum)
    totals = jnp.sum(raised, axis=-1, keepdims=True)
    attn_probs = (raised / totals).astype(BF16)
    mixed = jnp.einsum(
        "hqk,khd->qhd", attn_probs, split_heads(value_flat), preferred_element_type=F32
    ).astype(BF16)
    return mixed.reshape(query_flat.shape), (maximum + jnp.log(totals))[:, :, 0]


def attend_back(query_flat, key_flat, value_flat, mixed_flat, grad_flat, log_total, keep):
    queries, key_rows, value_rows, mixed, grad_mixed = map(
        split_heads, (query_flat, key_flat, value_flat, mixed_flat, grad_flat)
    )
    scores = masked_scores(queries, key_rows, keep)
    probs = jnp.exp(scores - log_total[:, :, None])
    grad_values = jnp.einsum(
        "hqk,qhd->khd", probs.astype(BF16), grad_mixed, preferred_element_type=F32
    )
    grad_probs = jnp.einsum("qhd,khd->hqk", grad_mixed, value_rows, preferred_element_type=F32)
    row_dots = jnp.sum(grad_mixed.astype(F32) * mixed.astype(F32), axis=-1).T[:, :, None]
    grad_scores = (probs * (grad_probs - row_dots)).astype(BF16)
    scale = HEAD_DIM ** (-0.5)
    grad_queries = (
        jnp.einsum("hqk,khd->qhd", grad_scores, key_rows, preferred_element_type=F32) * scale
    )
    grad_keys = (
        jnp.einsum("hqk,qhd->khd", grad_scores, queries, preferred_element_type=F32) * scale
    )
    flat = query_flat.shape
    return grad_queries.reshape(flat), grad_keys.reshape(flat), grad_values.reshape(flat)


def solution(mesh):
    tensor = mesh.shape["tensor"]
    dp = mesh.shape["dp"]
    ny, nx = 2, dp // 4
    places = ny * nx
    grid = Mesh(mesh.devices.reshape(ny, nx, 2, tensor), ("y", "x", "core", "tensor"))
    owners = ("y", "x", "core")

    def local(
        inputs,
        grad_output,
        valid_count,
        attend_weight,
        attend_bias,
        merge_weight,
        expand_weight,
        expand_bias,
        reduce_weight,
        norm_gains,
        norm_shifts,
        layer_scales,
        branch_biases,
    ):
        rows = inputs.shape[1]
        width = inputs.shape[2]
        seq = rows * tensor
        heads_width = attend_weight.shape[2]
        wide = width // places
        grad_scale = 1.0 / math.sqrt(dp * seq)
        core = lax.axis_index("core")
        place = lax.axis_index("y") * nx + lax.axis_index("x")
        dp_index = place * 2 + core
        lane = lax.axis_index("tensor")

        def reorder(value):
            return jnp.concatenate(
                [
                    lax.dynamic_slice_in_dim(value, (place ^ s) * wide, wide, value.ndim - 1)
                    for s in range(places)
                ],
                axis=-1,
            )

        def by_core(own, other, dim):
            return jnp.where(
                core == 0,
                jnp.concatenate([own, other], dim),
                jnp.concatenate([other, own], dim),
            )

        def halves(value, dim):
            half = value.shape[dim] // 2
            return (
                lax.dynamic_slice_in_dim(value, core * half, half, dim),
                lax.dynamic_slice_in_dim(value, (1 - core) * half, half, dim),
            )

        def core_swap(value):
            return swap(value, "core", 2, 1)

        def x_gather(value, dim):
            return jnp.concatenate(gather_relative(value, "x", nx), dim)

        def y_gather(value, dim):
            return jnp.concatenate(gather_relative(value, "y", ny), dim)

        packed = jnp.concatenate(
            [
                jnp.concatenate([norm_gains, norm_shifts, layer_scales, branch_biases]).reshape(-1),
                attend_bias.astype(F32).reshape(-1),
                expand_bias.astype(F32).reshape(-1),
            ]
        )
        part = norm_gains.shape[1]
        bias_part = attend_bias.shape[1]
        packed = lax.all_gather(lax.all_gather(packed, "tensor"), owners)
        vectors = (
            packed[:, :, : 8 * part]
            .reshape(dp, tensor, 8, part)
            .transpose(2, 0, 1, 3)
            .reshape(8, width)
        )
        vectors = reorder(vectors)
        own_lane = lax.dynamic_index_in_dim(
            packed[:, :, 8 * part : 8 * part + 2 * bias_part], lane, 1, keepdims=False
        )
        bias_own = own_lane.reshape(dp, 2, bias_part).transpose(1, 0, 2).reshape(2, heads_width)
        hidden_quarter = expand_bias.shape[0] * dp
        hidden_half = hidden_quarter // 2
        expand_bias_all = (
            packed[:, :, 8 * part + 2 * bias_part :].transpose(1, 0, 2).reshape(tensor * 2, hidden_half)
        )
        expand_bias_core = jnp.concatenate(
            [
                lax.dynamic_index_in_dim(
                    expand_bias_all, (lane ^ s) * 2 + core, 0, keepdims=False
                )
                for s in range(tensor)
            ]
        )

        attend_local = attend_weight.transpose(1, 0, 2).reshape(-1, 3 * heads_width)
        attend_pair = by_core(attend_local, core_swap(attend_local), 0)
        attend_own = y_gather(x_gather(attend_pair, 0), 0)

        x_rows = reorder(inputs[0])
        g_rows = reorder(grad_output[0])
        scaled_one, inverse_one = standardize(x_rows)
        rows_local = (scaled_one * vectors[0] + vectors[2]).astype(BF16)
        rows_one = jnp.concatenate(gather_line(rows_local, tensor), 0)

        merge_z = jnp.concatenate(gather_relative(merge_weight, "tensor", tensor), 0)
        merge_all = y_gather(x_gather(by_core(merge_z, core_swap(merge_z), 1), 1), 1)

        expand_own, expand_send = halves(expand_weight, 1)
        expand_pair = by_core(expand_own, core_swap(expand_send), 0)
        expand_z = jnp.concatenate(gather_relative(expand_pair, "tensor", tensor), 1)
        expand_all = y_gather(x_gather(expand_z, 0), 0)

        reduce_own, reduce_send = halves(reduce_weight, 0)
        reduce_pair = by_core(reduce_own, core_swap(reduce_send), 1)
        reduce_z = jnp.concatenate(gather_relative(reduce_pair, "tensor", tensor), 0)
        reduce_y = [gather_relative(v, "x", nx) for v in gather_relative(reduce_z, "y", ny)]
        reduce_all = jnp.concatenate([v for group in reduce_y for v in group], 1)

        attend_far = jnp.concatenate(gather_relative(attend_local, "tensor", tensor)[1:], 1)
        attend_far = y_gather(x_gather(by_core(attend_far, core_swap(attend_far), 0), 0), 0)

        query_bias = jnp.concatenate(
            [bias_own[0], jnp.zeros_like(bias_own[0]), bias_own[1]]
        )
        projected = (dot(rows_one, attend_own, 1, 0) + query_bias).astype(BF16)
        q_flat, k_flat, v_flat = (
            projected[:, i * heads_width : (i + 1) * heads_width] for i in range(3)
        )
        position = jnp.concatenate(
            [(lane ^ s) * rows + jnp.arange(rows, dtype=jnp.int32) for s in range(tensor)]
        )
        keep = position < valid_count[0]
        mixed_own, log_total = attend(q_flat, k_flat, v_flat, keep)
        mixed = jnp.concatenate(
            exchange([mixed_own[s * rows : (s + 1) * rows] for s in range(tensor)], "tensor", tensor),
            1,
        )
        branch_one = dot(mixed, merge_all, 1, 0) + vectors[6]
        middle = x_rows + vectors[4] * branch_one
        scaled_two, inverse_two = standardize(middle)
        rows_two = (scaled_two * vectors[1] + vectors[3]).astype(BF16)
        grad_two = (g_rows * vectors[5]).astype(BF16)

        grad_two_pair = jnp.concatenate([grad_two, core_swap(grad_two)], 0)
        rows_two_pair = jnp.concatenate([rows_two, core_swap(rows_two)], 0)
        pre_act = dot(rows_two_pair, expand_all, 1, 0) + expand_bias_core
        hidden = jax.nn.gelu(pre_act, approximate=False).astype(BF16)
        two_part = dot(hidden, reduce_all, 1, 0)
        branch_two = two_part[:rows] + core_swap(two_part[rows:]) + vectors[7]
        layer_output = middle + vectors[5] * branch_two
        reduce_part = dot(hidden, grad_two_pair, 0, 0).astype(BF16)
        grad_pre = dot(grad_two_pair, reduce_all, 1, 1) * gelu_slope(pre_act)
        grad_pre_low = grad_pre.astype(BF16)
        expand_part = dot(rows_two_pair, grad_pre_low, 0, 0).astype(BF16)
        expand_bias_part = jnp.sum(grad_pre, axis=0)
        norm_two_part = dot(grad_pre_low, expand_all, 1, 1)
        grad_norm_two = norm_two_part[:rows] + core_swap(norm_two_part[rows:])
        grad_middle = g_rows + norm_back(grad_norm_two, scaled_two, inverse_two, vectors[1])
        grad_one = (grad_middle * vectors[4]).astype(BF16)
        merge_part = dot(mixed, grad_one, 0, 0).astype(BF16)
        grad_mixed = dot(grad_one, merge_all, 1, 1).astype(BF16)
        grad_mixed_own = jnp.concatenate(
            exchange(
                [grad_mixed[:, s * heads_width : (s + 1) * heads_width] for s in range(tensor)],
                "tensor",
                tensor,
            ),
            0,
        )
        grads_qkv = attend_back(
            q_flat, k_flat, v_flat, mixed_own, grad_mixed_own, log_total, keep
        )
        attend_bias_part = jnp.stack([jnp.sum(grads_qkv[0], 0), jnp.sum(grads_qkv[2], 0)])
        grad_low = jnp.concatenate([g.astype(BF16) for g in grads_qkv], 1)
        attend_part = dot(rows_one, grad_low, 0, 0).astype(BF16)
        grad_far = exchange([grad_low[s * rows : (s + 1) * rows] for s in range(tensor)], "tensor", tensor)
        grad_norm_one = dot(grad_far[0], attend_own, 1, 1) + dot(
            jnp.concatenate(grad_far[1:], 1), attend_far, 1, 1
        )
        input_grad = grad_middle + norm_back(
            grad_norm_one, scaled_one, inverse_one, vectors[0]
        )

        def x_scatter(value, dim):
            size = value.shape[dim] // nx
            chunks = [lax.slice_in_dim(value, s * size, (s + 1) * size, axis=dim) for s in range(nx)]
            return add_up(exchange(chunks, "x", nx)).astype(BF16)

        def y_scatter(value, dim):
            size = value.shape[dim] // ny
            chunks = [lax.slice_in_dim(value, s * size, (s + 1) * size, axis=dim) for s in range(ny)]
            return add_up(exchange(chunks, "y", ny)).astype(BF16)

        def z_scatter(value, dim):
            size = value.shape[dim] // tensor
            chunks = [
                lax.slice_in_dim(value, s * size, (s + 1) * size, axis=dim) for s in range(tensor)
            ]
            return add_up(exchange(chunks, "tensor", tensor))

        def core_scatter(value, dim):
            own, other = halves(value, dim)
            return add_up([own, core_swap(other)])

        reduce_sum = x_scatter(
            reduce_part.reshape(-1, ny, nx, wide).transpose(0, 2, 1, 3).reshape(-1, width), 1
        )
        reduce_sum = z_scatter(y_scatter(reduce_sum, 1), 0)
        reduce_keep, reduce_give = halves(reduce_sum, 1)
        reduce_grad = by_core(reduce_keep, core_swap(reduce_give), 0) * grad_scale

        expand_sum = z_scatter(x_scatter(y_scatter(expand_part, 0), 0), 1)
        expand_keep, expand_give = halves(expand_sum, 0)
        expand_grad = by_core(expand_keep, core_swap(expand_give), 1) * grad_scale

        merge_sum = x_scatter(y_scatter(merge_part, 1), 1)
        merge_sum = core_scatter(merge_sum, 1).astype(BF16)
        merge_grad = z_scatter(merge_sum, 0) * grad_scale

        attend_sum = x_scatter(y_scatter(attend_part, 0), 0)
        attend_grad = core_scatter(attend_sum, 0) * grad_scale
        attend_grad = attend_grad.reshape(-1, 3, heads_width).transpose(1, 0, 2)

        def token_sum(value):
            return jnp.sum(value, axis=0)

        sums = reorder(
            jnp.stack(
                [
                    token_sum(grad_norm_one * scaled_one),
                    token_sum(grad_norm_two * scaled_two),
                    token_sum(grad_norm_one),
                    token_sum(grad_norm_two),
                    token_sum(grad_middle * branch_one),
                    token_sum(g_rows * branch_two),
                    token_sum(grad_middle * vectors[4]),
                    token_sum(g_rows * vectors[5]),
                ]
            )
        )
        hidden_sums = jnp.zeros((tensor * 2, hidden_half), F32)
        for s in range(tensor):
            hidden_sums = lax.dynamic_update_slice_in_dim(
                hidden_sums,
                expand_bias_part[None, s * hidden_half : (s + 1) * hidden_half],
                (lane ^ s) * 2 + core,
                0,
            )
        bias_sums = lax.dynamic_update_slice_in_dim(
            jnp.zeros((2, width), F32), attend_bias_part, lane * heads_width, 1
        )
        small = jnp.concatenate([sums.reshape(-1), hidden_sums.reshape(-1), bias_sums.reshape(-1)])
        small = small.reshape(-1, 128)
        small = small + core_swap(small)
        for axis, size in (("x", nx), ("y", ny), ("tensor", tensor)):
            distance = 1
            while distance < size:
                small = small + swap(small, axis, size, distance)
                distance *= 2
        small = small.reshape(-1) * grad_scale
        vector_grads = lax.dynamic_slice_in_dim(
            small[: 8 * width].reshape(8, width), (dp_index * tensor + lane) * part, part, 1
        )
        expand_bias_grad = lax.dynamic_slice_in_dim(
            small, 8 * width + (lane * dp + dp_index) * expand_bias.shape[0], expand_bias.shape[0], 0
        )
        attend_bias_grad = lax.dynamic_slice_in_dim(
            small[-2 * width :].reshape(2, width), (lane * dp + dp_index) * bias_part, bias_part, 1
        )
        return (
            reorder(layer_output)[None],
            reorder(input_grad)[None],
            attend_grad,
            attend_bias_grad,
            merge_grad,
            expand_grad,
            expand_bias_grad,
            reduce_grad,
            vector_grads[0:2],
            vector_grads[2:4],
            vector_grads[4:6],
            vector_grads[6:8],
        )

    rows_spec = P(owners, "tensor", None)
    by_owner = P(None, owners + ("tensor",))
    by_tensor = ("tensor",) + owners
    return jax.shard_map(
        local,
        mesh=grid,
        in_specs=(
            rows_spec,
            rows_spec,
            P(owners),
            P(None, owners, "tensor"),
            P(None, by_tensor),
            P("tensor", owners),
            P(owners, "tensor"),
            P(by_tensor),
            P("tensor", owners),
            by_owner,
            by_owner,
            by_owner,
            by_owner,
        ),
        out_specs=(
            rows_spec,
            rows_spec,
            P(None, owners, "tensor"),
            P(None, by_tensor),
            P("tensor", owners),
            P(owners, "tensor"),
            P(by_tensor),
            P("tensor", owners),
            by_owner,
            by_owner,
            by_owner,
            by_owner,
        ),
        check_vma=False,
    )
```
